32 devices in a mesh: freq: 8 (over z, x), pol: 2 (over core), beam: 2 (over y).
Axes of the slice: x: 2, y: 2, z: 4, core: 2. Of those that a mesh axis runs over, the one named last changes fastest.
Arguments:
- voltages: bfloat16 [1024, 2, 256, 512], P('freq', 'pol', 'beam'), may hold values from -6 to 6
- beam_weights: bfloat16 [256, 2, 1024, 512], P('freq', None, None, 'beam'), may hold values from -0.125 to 0.125
- delay_shifts: int32 [8, 256], replicated, may hold values from 0 to 255, as said below
Outputs:
- dedispersed: float32 [256, 2, 256, 256], P('freq', 'beam', 'pol')
The draws below stay inside these ranges and needn't reach their ends.
Inputs may be any that keep to these rules, and one draw needn't show every extreme that they name: delay_shifts[s, d] lies between (d + 1) // 2 and d; only entries with d below 2 ** (s + 1) are read.
All inputs are finite; a program needn't handle non-finite values.
Results may differ from the reference program's by a relative error of at most 0.0006.
Values may be sent and summed in bfloat16 or wider, within the bound.
A program may use at most 256 MiB of HBM per device.

```python
import math
import jax
import jax.numpy as jnp
import numpy as np
from jax import lax

ANTENNAS = 1024
F = 256
BEAMS = 512
POLS = 2
LEVELS = 8
SPECTRA = 256
N_FREQ = 8
N_BEAM = 2


def draw_delay_shifts(key, part):
    delay_ids = jnp.broadcast_to(jnp.arange(F, dtype=jnp.int32)[None, :], (LEVELS, F))
    lowest = (delay_ids + 1) // 2
    drawn = jax.random.randint(key, (LEVELS, F), lowest, delay_ids + 1, dtype=jnp.int32)
    drawn = jnp.where(delay_ids == F - 1, F - 1, drawn)
    return drawn.astype(jnp.int32)


def level_of(stream_key, shape, pieces, least, high):
    def one(axis_at, parts):
        steps = jax.random.uniform(jax.random.fold_in(jax.random.fold_in(stream_key, 6), axis_at), (parts,), jnp.float32, least / len(pieces), high / len(pieces))
        return jnp.repeat(jnp.exp(steps), shape[axis_at] // parts).reshape((-1,) + (1,) * (len(shape) - axis_at - 1))

    factor_of = one(*pieces[0])
    for cut in pieces[1:]:
        factor_of = factor_of * one(*cut)
    return factor_of


def gaussian(rng, dims, width, limit, split=(), held_as=jnp.bfloat16):
    gain = level_of(rng, dims, split, -0.22, 0.18) if split else 1.0
    result = jax.random.normal(rng, dims, jnp.float32) * width * gain
    return jnp.minimum(jnp.maximum(result, -limit), limit).astype(held_as)


def setup_inputs(seed: int = 0) -> dict:
    seeds = jax.random.split(jax.random.key(seed), 4)
    return {
        "voltages": gaussian(seeds[0], (ANTENNAS, POLS, SPECTRA, 2 * F), 1.0, 6.0, ((0, 8), (1, 2), (2, 2))),
        "beam_weights": gaussian(seeds[1], (F, 2, ANTENNAS, BEAMS), (2 * ANTENNAS) ** -0.5, 0.125, ((0, 8), (3, 2))),
        "delay_shifts": draw_delay_shifts(jax.random.fold_in(seeds[3], 71), 0),
    }


def fourier_table(length):
    index_row = jnp.arange(length, dtype=jnp.int32)
    product = index_row[:, None] * index_row[None, :] % length
    phase_angle = 2.0 * math.pi / length * product.astype(jnp.float32)
    norm_scale = 1.0 / math.sqrt(length)
    cosine = jnp.cos(phase_angle) * norm_scale
    sine_part = jnp.sin(phase_angle) * norm_scale
    real_rows = jnp.concatenate([cosine, sine_part], axis=1)
    imag_rows = jnp.concatenate([-sine_part, cosine], axis=1)
    return jnp.concatenate([real_rows, imag_rows], axis=0).astype(jnp.bfloat16)

def shift_rows(planes, amounts):
    length = planes.shape[-1]
    padded = jnp.concatenate([planes, jnp.zeros_like(planes)], axis=-1)
    return jax.vmap(lambda single_plane, amount: lax.dynamic_slice_in_dim(single_plane, amount.astype(jnp.int32), length, axis=1))(padded, amounts)

def merge_level(planes, shift_row):
    first_half = planes[0::2]
    second_half = planes[1::2]
    widened = 2 * planes.shape[1]
    first_rep = jnp.repeat(first_half, 2, axis=1)
    second_rep = jnp.repeat(second_half, 2, axis=1)
    amounts = shift_row[:widened]
    shifted = jax.vmap(shift_rows, in_axes=(0, None))(second_rep, amounts)
    return first_rep + shifted

def slot_order(device_total, rows_each):
    level_bits = device_total.bit_length() - 1
    ordering = []
    for block_index in range(device_total):
        flipped = 0
        remainder = block_index
        for bit_index in range(level_bits):
            flipped = 2 * flipped + remainder % 2
            remainder = remainder // 2
        for row_index in range(rows_each):
            ordering.append(rows_each * flipped + row_index)
    return np.array(ordering, dtype=np.int32)

def reference(voltages, beam_weights, delay_shifts):
    fourier = fourier_table(F).astype(jnp.float32)
    wide_volts = voltages.astype(jnp.float32)

    def one_channel(channel):
        table_rows = jnp.stack([fourier[channel], fourier[F + channel]])
        channel_volts = jnp.einsum('pn,aqsn->paqs', table_rows, wide_volts)
        channel_volts = lax.optimization_barrier(channel_volts.astype(jnp.bfloat16)).astype(jnp.float32)
        channel_weights = beam_weights[channel].astype(jnp.float32)
        real_beam = jnp.einsum('ab,aqs->qbs', channel_weights[0], channel_volts[0]) - jnp.einsum('ab,aqs->qbs', channel_weights[1], channel_volts[1])
        imag_beam = jnp.einsum('ab,aqs->qbs', channel_weights[1], channel_volts[0]) + jnp.einsum('ab,aqs->qbs', channel_weights[0], channel_volts[1])
        return lax.optimization_barrier(jnp.sum(real_beam * real_beam + imag_beam * imag_beam, axis=0))
    beam_power = lax.map(one_channel, jnp.arange(F, dtype=jnp.int32))
    planes = beam_power[:, None]
    for level_index in range(LEVELS):
        planes = merge_level(planes, delay_shifts[level_index])
    delays = planes[0] * (1.0 / (4 * F))
    ordered = jnp.take(delays, jnp.asarray(slot_order(N_FREQ, F // N_FREQ)), axis=0)
    return ordered.reshape(F, N_BEAM, BEAMS // N_BEAM, SPECTRA)
```

```python
import functools
import math

import jax
import jax.numpy as jnp
from jax import lax
from jax.experimental import pallas as pl
from jax.experimental.pallas import tpu as pltpu
from jax.sharding import PartitionSpec as P

F = 256
PIECES = 2


def swapped(shard, axis, bit):
    return lax.ppermute(shard, axis, [(i, i ^ 1 << bit) for i in range(lax.axis_size(axis))])


def fourier_table(length):
    index_row = jnp.arange(length, dtype=jnp.int32)
    product = index_row[:, None] * index_row[None, :] % length
    phase_angle = 2.0 * math.pi / length * product.astype(jnp.float32)
    norm_scale = 1.0 / math.sqrt(length)
    cosine = jnp.cos(phase_angle) * norm_scale
    sine_part = jnp.sin(phase_angle) * norm_scale
    real_rows = jnp.concatenate([cosine, sine_part], axis=1)
    imag_rows = jnp.concatenate([-sine_part, cosine], axis=1)
    return jnp.concatenate([real_rows, imag_rows], axis=0).astype(jnp.bfloat16)


def antenna_rows(ref, part):
    block = ref[:, part, 0]
    sources, antennas, length = block.shape
    if antennas % 16 == 0:
        return block.reshape(sources * antennas, length)
    wide = block.astype(jnp.float32).reshape(sources * antennas, length)
    return wide.astype(block.dtype)


def over_antennas(volts, weights):
    return lax.dot_general(
        volts, weights, (((0,), (0,)), ((), ())), preferred_element_type=jnp.float32
    )


def power_kernel(own_volts, other_volts, own_weights, other_weights, own_power, other_power):
    real_volts = jnp.concatenate([antenna_rows(own_volts, 0), antenna_rows(other_volts, 0)], axis=1)
    imag_volts = jnp.concatenate([antenna_rows(own_volts, 1), antenna_rows(other_volts, 1)], axis=1)
    real_weights = jnp.concatenate([own_weights[0, 0], other_weights[0, 0]], axis=1)
    imag_weights = jnp.concatenate([own_weights[0, 1], other_weights[0, 1]], axis=1)
    real_beam = over_antennas(real_volts, real_weights) - over_antennas(imag_volts, imag_weights)
    imag_beam = over_antennas(real_volts, imag_weights) + over_antennas(imag_volts, real_weights)
    both = real_beam * real_beam + imag_beam * imag_beam
    half = both.shape[0] // 2
    power = both[:half] + both[half:]
    beams = own_weights.shape[3]
    own_power[0] = power[:, :beams]
    other_power[0] = power[:, beams:].astype(other_power.dtype)


def beam_power(own_volts, other_volts, own_weights, other_weights, offset):
    sources, _, channels, antennas, length = own_volts.shape
    beams = own_weights.shape[3]
    volt_spec = pl.BlockSpec((sources, 2, 1, antennas, length), lambda c: (0, 0, c, 0, 0))
    weight_spec = pl.BlockSpec(
        (1, 2, own_weights.shape[2], beams), lambda c: (c + offset, 0, 0, 0)
    )
    power_spec = pl.BlockSpec((1, length, beams), lambda c: (c, 0, 0))
    macs = channels * sources * antennas * length * beams * 16
    return pl.pallas_call(
        power_kernel,
        grid=(channels,),
        in_specs=[volt_spec, volt_spec, weight_spec, weight_spec],
        out_specs=[power_spec, power_spec],
        out_shape=[
            jax.ShapeDtypeStruct((channels, length, beams), jnp.float32),
            jax.ShapeDtypeStruct((channels, length, beams), jnp.bfloat16),
        ],
        compiler_params=pltpu.CompilerParams(vmem_limit_bytes=40 * 2**20),
        cost_estimate=pl.CostEstimate(
            flops=2 * macs, bytes_accessed=2 * own_volts.size * 4, transcendentals=0
        ),
    )(own_volts, other_volts, own_weights, other_weights)


def emit_rows(make_row, half_rows, high, keep_ref, send_ref):
    def body(row, carry):
        keep_ref[row] = make_row(high * half_rows + row)
        send_ref[row] = make_row((1 - high) * half_rows + row)
        return carry

    lax.fori_loop(0, half_rows, body, 0)


def tree_kernel(levels, info, shifts, own, other, keep_ref, send_ref, ping, pong):
    channels, part, _ = own.shape
    length = 2 * part
    side = info[0]
    device = info[1]
    ping[:, length:] = jnp.zeros_like(ping[:, length:])
    pong[:, length:] = jnp.zeros_like(pong[:, length:])

    def fill(row, carry):
        ping[row, pl.ds(pl.multiple_of(side * part, 8), part)] = own[row]
        ping[row, pl.ds(pl.multiple_of((1 - side) * part, 8), part)] = other[row].astype(jnp.float32)
        return carry

    lax.fori_loop(0, channels, fill, 0)
    source, target = ping, pong
    for level in range(levels):

        def make_row(row, source=source, level=level):
            group = row >> (level + 1)
            delay = row & ((2 << level) - 1)
            first = (2 * group << level) + (delay >> 1)
            second = first + (1 << level)
            return source[first, :length] + source[second, pl.ds(shifts[level, delay], length)]

        if level < levels - 1:

            def body(row, carry, make_row=make_row, target=target):
                target[row, :length] = make_row(row)
                return carry

            lax.fori_loop(0, channels, body, 0)
            source, target = target, source
        else:
            emit_rows(make_row, channels // 2, device & 1, keep_ref, send_ref)


def section_kernel(section, sections, level, scale, info, shifts, kept, received, *rest):
    outs, held = rest[:-1], rest[-1]
    half_rows, length, _ = kept.shape
    rows = 2 * half_rows
    device = info[1]
    high = (device >> section) & 1
    position = 0
    for bit in range(section + 1):
        position = 2 * position + ((device >> bit) & 1)
    held[:, :, length:] = jnp.zeros_like(held[:, :, length:])

    def fill(row, carry):
        held[high, row, :length] = kept[row]
        held[1 - high, row, :length] = received[row]
        return carry

    lax.fori_loop(0, half_rows, fill, 0)

    def make_row(row):
        amount = shifts[level, position * rows + row]
        return held[0, row >> 1, :length] + held[1, row >> 1, pl.ds(amount, length)]

    if section + 1 < sections:
        emit_rows(make_row, half_rows, (device >> (section + 1)) & 1, *outs)
    else:

        def body(row, carry):
            outs[0][row] = jnp.transpose(make_row(row) * scale)
            return carry

        lax.fori_loop(0, rows, body, 0)


SMEM_SPEC = pl.BlockSpec(memory_space=pltpu.SMEM)
VMEM_SPEC = pl.BlockSpec(memory_space=pltpu.VMEM)


def per_device(voltages, beam_weights, delay_shifts):
    sources = lax.axis_size("freq")
    rows_each = beam_weights.shape[0]
    beams = beam_weights.shape[3] // lax.axis_size("pol")
    antennas, _, spectra, samples = voltages.shape
    device = lax.axis_index("freq")
    side = lax.axis_index("beam")
    core = lax.axis_index("pol")
    info = jnp.stack([side, device]).astype(jnp.int32)

    own_weights = lax.dynamic_slice_in_dim(beam_weights, core * beams, beams, axis=3)
    other_weights = swapped(own_weights, "beam", 0)

    pieces = PIECES if rows_each % PIECES == 0 else 1
    each = rows_each // pieces
    table = fourier_table(F).reshape(2, sources, rows_each, samples).transpose(1, 0, 2, 3)
    own_parts, other_parts = [], []
    turned_parts = []
    for piece in range(pieces):
        rows = table[:, :, piece * each : (piece + 1) * each].reshape(-1, samples)
        channelized = lax.dot_general(
            rows, voltages[:, 0], (((1,), (2,)), ((), ())), preferred_element_type=jnp.float32
        )
        channelized = channelized.astype(jnp.bfloat16).reshape(
            sources, 2, each, antennas, spectra
        )
        turned = lax.all_to_all(channelized, "freq", split_axis=0, concat_axis=0)
        turned_parts.append((turned, swapped(turned, "pol", 0)))
    for piece, (turned, other_turned) in enumerate(turned_parts):
        own, other = beam_power(turned, other_turned, own_weights, other_weights, piece * each)
        own_parts.append(own)
        other_parts.append(swapped(other, "beam", 0))
    own_power = jnp.concatenate(own_parts, axis=0)
    other_power = jnp.concatenate(other_parts, axis=0)

    length = 2 * spectra
    levels = rows_each.bit_length() - 1
    sections = sources.bit_length() - 1
    half = jax.ShapeDtypeStruct((rows_each // 2, length, beams), jnp.float32)
    kept, sent = pl.pallas_call(
        functools.partial(tree_kernel, levels),
        in_specs=[SMEM_SPEC, SMEM_SPEC, VMEM_SPEC, VMEM_SPEC],
        out_specs=[VMEM_SPEC, VMEM_SPEC],
        out_shape=[half, half],
        scratch_shapes=[pltpu.VMEM((rows_each, 2 * length, beams), jnp.float32)] * 2,
        compiler_params=pltpu.CompilerParams(vmem_limit_bytes=40 * 2**20),
    )(info, delay_shifts, own_power, other_power)
    for section in range(sections):
        received = swapped(sent, "freq", section)
        last = section + 1 == sections
        shape = [jax.ShapeDtypeStruct((rows_each, beams, length), jnp.float32)] if last else [half] * 2
        result = pl.pallas_call(
            functools.partial(
                section_kernel, section, sections, levels + section, 1.0 / (4 * F)
            ),
            in_specs=[SMEM_SPEC, SMEM_SPEC, VMEM_SPEC, VMEM_SPEC],
            out_specs=[VMEM_SPEC] * len(shape),
            out_shape=shape,
            scratch_shapes=[pltpu.VMEM((2, rows_each // 2, 2 * length, beams), jnp.float32)],
            compiler_params=pltpu.CompilerParams(vmem_limit_bytes=40 * 2**20),
        )(info, delay_shifts, kept, received)
        if last:
            return result[0][:, None]
        kept, sent = result


def solution(mesh):
    in_specs = (P("freq", "pol", "beam", None), P("freq", None, None, "beam"), P())
    out_specs = P("freq", "beam", "pol", None)
    return jax.shard_map(
        per_device, mesh=mesh, in_specs=in_specs, out_specs=out_specs, check_vma=False
    )
```
